32 devices in a mesh: replica: 8 (over z, y), fsdp: 4 (over x, core).
Axes of the slice: x: 2, y: 2, z: 4, core: 2. Of those that a mesh axis runs over, the one named last changes fastest.
Arguments:
- inner_weights: bfloat16 [8, 4, 1024, 8192], P('replica', None, 'fsdp'), may hold values from -6 to 6
- snapshot: bfloat16 [1024, 8192], P('fsdp'), may hold values from -6 to 6
- momentum: float32 [1024, 8192], P('fsdp', 'replica'), may hold values from -6 to 6
- rand_bits: int32 [8, 1024, 8192], P('replica', 'fsdp'), may hold values from 0 to 4095
- fragment: int32 [1], replicated, may hold values from 0 to 3
Outputs:
- new_snapshot: bfloat16 [1024, 8192], P('fsdp')
- new_momentum: float32 [1024, 8192], P('fsdp', 'replica')
- new_inner: bfloat16 [8, 4, 1024, 8192], P('replica', None, 'fsdp')
The draws below stay inside these ranges and needn't reach their ends.
Inputs may be any that keep to these rules, and one draw needn't show every extreme that they name: fragment[0] is one of 0, 1, 2, 3, the fragment of the window that syncs.
All inputs are finite; a program needn't handle non-finite values.
Results may differ from the reference program's by a relative error of at most 0.0075.
Values may be sent and summed in bfloat16 or wider, within the bound.
A program may use at most 128 MiB of HBM per device.

```python
import jax
import jax.numpy as jnp
from jax import lax

D = 8192
KV = 1024
FRAGS = 4
REPLICAS = 8


def touch_ends(result, stream_key, smallest, high):
    longest = result.shape.index(max(result.shape))
    spots = []
    for shift in (0, 1):
        where = [jax.random.randint(jax.random.fold_in(stream_key, axis), (), 0, length) for axis, length in enumerate(result.shape)]
        where[longest] = (where[longest] + shift) % result.shape[longest]
        spots.append(tuple(where))
    return result.at[spots[0]].set(smallest).at[spots[1]].set(high)


def level_of(rng, dims, cuts, smallest, high):
    def one(position, parts):
        steps = jax.random.uniform(jax.random.fold_in(jax.random.fold_in(rng, 6), position), (parts,), jnp.float32, smallest / len(cuts), high / len(cuts))
        return jnp.repeat(jnp.exp(steps), dims[position] // parts).reshape((-1,) + (1,) * (len(dims) - position - 1))

    gain = one(*cuts[0])
    for cut in cuts[1:]:
        gain = gain * one(*cut)
    return gain


def gaussian(rng, extent, width, limit, split=(), kind=jnp.bfloat16):
    level = level_of(rng, extent, split, -0.22, 0.18) if split else 1.0
    result = jax.random.normal(rng, extent, jnp.float32) * width * level
    return jnp.minimum(jnp.maximum(result, -limit), limit).astype(kind)


def setup_inputs(seed: int = 0) -> dict:
    seeds = jax.random.split(jax.random.key(seed), 6)
    inner_weights = gaussian(seeds[0], (REPLICAS, FRAGS, KV, D), 1.0, 6.0, ((0, 8), (2, 4)))
    snapshot = gaussian(seeds[1], (KV, D), 1.0, 6.0, ((0, 4),))
    momentum = gaussian(seeds[2], (KV, D), 1.0, 6.0, ((0, 4), (1, 8)), jnp.float32)
    rand_bits = touch_ends(jax.random.randint(seeds[3], (REPLICAS, KV, D), 0, 4096), jax.random.fold_in(seeds[3], 1), 0, 4095).astype(jnp.int32)
    fragment = jax.random.randint(seeds[4], (1,), 0, FRAGS).astype(jnp.int32)
    return {"inner_weights": inner_weights, "snapshot": snapshot, "momentum": momentum, "rand_bits": rand_bits, "fragment": fragment}


momentum_coef = 0.9
outer_rate = 0.7
blend_keep = 0.5
grid_scale = 4.0
bit_levels = 4096.0


def stochastic_grid(snapshot, chosen, rand_bits):
    scaled = grid_scale * (snapshot.astype(jnp.float32) - chosen.astype(jnp.float32))
    lower = jnp.floor(scaled)
    raised = jnp.where(rand_bits.astype(jnp.float32) < bit_levels * (scaled - lower), 1.0, 0.0).astype(jnp.float32)
    return ((lower + raised) / grid_scale).astype(jnp.bfloat16)


def reference(inner_weights, snapshot, momentum, rand_bits, fragment):
    fragment_id = fragment[0].astype(jnp.int32)
    chosen_all = lax.dynamic_index_in_dim(inner_weights, fragment_id, 1, keepdims=False)

    def accumulate(summed, pair):
        chosen, bits = pair
        return summed + stochastic_grid(snapshot, chosen, bits).astype(jnp.float32), None

    summed, _ = lax.scan(accumulate, jnp.zeros(snapshot.shape, jnp.float32), (chosen_all, rand_bits))
    grad = summed / REPLICAS
    new_momentum = momentum_coef * momentum + grad
    new_snapshot = (snapshot.astype(jnp.float32) - outer_rate * (grad + momentum_coef * new_momentum)).astype(jnp.bfloat16)
    blended = (blend_keep * chosen_all.astype(jnp.float32) + (1.0 - blend_keep) * new_snapshot.astype(jnp.float32)[None]).astype(jnp.bfloat16)
    picked = lax.broadcasted_iota(jnp.int32, (1, FRAGS, 1, 1), 1) == fragment_id
    new_inner = jnp.where(picked, blended[:, None], inner_weights)
    return new_snapshot, new_momentum, new_inner
```

```python
import functools

import jax
import jax.numpy as jnp
from jax import lax
from jax.experimental import pallas as pl
from jax.experimental.pallas import tpu as pltpu
from jax.sharding import PartitionSpec as P

momentum_coef = 0.9
outer_rate = 0.7
blend_keep = 0.5
grid_scale = 4.0
bit_levels = 4096.0
MESH = pl.DeviceIdType.MESH
CHUNK_ROWS = 32
TUNED = [(2, 1, 2), (8, 0, 14), (7, 0, 9), (-1, 0, 0), (4, 1, 3), (4, 0, 4), (0, 1, 0), (5, 0, 5), (7, 1, 12), (8, 1, 23), (3, 1, 2), (6, 0, 6), (0, 0, 0), (1, 1, 1), (3, 0, 3), (6, 1, 4), (5, 1, 3), (1, 0, 1), (2, 0, 2)]
EXCHANGE_VMEM = 42 << 20
FINISH_VMEM = 10 << 20


def when(cond):
    if isinstance(cond, bool):
        return (lambda f: f()) if cond else (lambda f: None)
    return pl.when(cond)


def grid_of(n):
    inner = max(k for k in range(1, n + 1) if n % k == 0 and k * k <= n)
    return n // inner, inner


def order_of(stages):
    if stages == max(s for s, _, _ in TUNED) + 1:
        return TUNED
    older = [(s, part, s) for s in range(stages - 1, 0, -1) for part in (0, 1)]
    return [*older, (-1, 0, 0), (0, 0, 0), (0, 1, 0)]


class Part:
    def __init__(self, bufs, sems, line1, line2, me, cols, width, draining):
        self.own, self.r1, self.l1, self.r2, self.l2, self.res = bufs
        (self.s1, self.sr1, self.sl1, self.s2, self.sr2, self.sl2,
         self.g2, self.g2r, self.g2l, self.g1, self.g1r, self.g1l) = sems
        (self.p1, self.n1, self.d1) = line1
        (self.p2, self.n2, self.d2) = line2
        self.me, self.cols, self.width = me, cols, width
        self.top = self.n1 + self.n2 - 2
        self.last = 2 * self.top
        self.draining = draining

    def send(self, src, dst, send_sem, recv_sem, delta):
        copy = pltpu.make_async_remote_copy(
            src_ref=src, dst_ref=dst, send_sem=send_sem, recv_sem=recv_sem,
            device_id={"replica": self.me + delta}, device_id_type=MESH,
        )
        if self.draining:
            copy.wait_send()
        else:
            copy.start()

    def arrive(self, dst, recv_sem):
        if not self.draining:
            pltpu.make_async_remote_copy(
                src_ref=dst, dst_ref=dst, send_sem=recv_sem, recv_sem=recv_sem,
                device_id={"replica": self.me}, device_id_type=MESH,
            ).wait_recv()

    def add1(self, c, q, recv):
        if not self.draining:
            for i in range(self.n2):
                self.own[c, q, i] = self.own[c, q, i] + recv[c, q, i]

    def add2(self, c, q, recv):
        if not self.draining:
            self.own[c, self.p1, q] = self.own[c, self.p1, q] + recv[c, q]

    def send1(self, c, q, right):
        recv, sem, delta = (self.r1, self.sr1, self.d1) if right else (self.l1, self.sl1, -self.d1)
        self.send(self.own.at[c, q], recv.at[c, q], self.s1.at[c, q], sem.at[c, q], delta)

    def send2(self, c, q, right):
        recv, sem, delta = (self.r2, self.sr2, self.d2) if right else (self.l2, self.sl2, -self.d2)
        self.send(self.own.at[c, self.p1, q], recv.at[c, q], self.s2.at[c, q], sem.at[c, q], delta)

    def gsend2(self, c, q, right):
        sem, delta = (self.g2r, self.d2) if right else (self.g2l, -self.d2)
        block = self.res.at[c, self.p1, q]
        self.send(block, block, sem.at[c, q], self.g2.at[c, q], delta)

    def gsend1(self, c, q1, q2, right):
        sem, delta = (self.g1r, self.d1) if right else (self.g1l, -self.d1)
        block = self.res.at[c, q1, q2]
        self.send(block, block, sem.at[c, q1, q2], self.g1.at[c, q1, q2], delta)

    def spread1(self, c, q2):
        p1 = self.p1
        when(p1 < self.n1 - 1)(lambda: self.gsend1(c, p1, q2, True))
        when(p1 > 0)(lambda: self.gsend1(c, p1, q2, False))

    def reduce_line(self, c, h, p, n, send, arrived, recvs, sems, add):
        right_recv, left_recv = recvs
        right_sem, left_sem = sems

        @when(p == h)
        def _():
            for q in range(n - 1, h - (h > 0), -1):
                if h > 0:
                    self.arrive(right_recv.at[c, q], right_sem.at[c, q])
                    if q > h or arrived:
                        add(c, q, right_recv)
                if q > h:
                    send(c, q, True)

        e = n - 1 - h

        @when(p == e)
        def _():
            for q in range(0, e + (h > 0)):
                if h > 0:
                    self.arrive(left_recv.at[c, q], left_sem.at[c, q])
                    if q < e or arrived:
                        add(c, q, left_recv)
                if q < e:
                    send(c, q, False)

    def hop1(self, s, c):
        if s < self.n1:
            self.reduce_line(c, s, self.p1, self.n1, self.send1, True, (self.r1, self.l1), (self.sr1, self.sl1), self.add1)

    def hop2(self, s, c):
        h = s - (self.n1 - 1)
        if 0 <= h < self.n2:
            self.reduce_line(c, h, self.p2, self.n2, self.send2, False, (self.r2, self.l2), (self.sr2, self.sl2), self.add2)

    def update(self, c, snap, mom, mom_next, acc, replicas, share):
        p1, p2 = self.p1, self.p2
        if not self.draining:
            acc[...] = self.own[c, p1, p2].astype(jnp.float32)

            @when(p2 > 0)
            def _():
                acc[...] += self.r2[c, p2].astype(jnp.float32)

            @when(p2 < self.n2 - 1)
            def _():
                acc[...] += self.l2[c, p2].astype(jnp.float32)

            start = self.me * share + self.cols
            if not isinstance(start, int):
                start = pl.multiple_of(start, 128)
            here = pl.ds(self.cols, self.width)
            grad = acc[...] / replicas
            moment = momentum_coef * mom[c, :, here] + grad
            mom_next[c, :, here] = moment
            base = snap[c, :, pl.ds(start, self.width)].astype(jnp.float32)
            self.res[c, p1, p2] = (base - outer_rate * (grad + momentum_coef * moment)).astype(jnp.bfloat16)
        when(p2 < self.n2 - 1)(lambda: self.gsend2(c, p2, True))
        when(p2 > 0)(lambda: self.gsend2(c, p2, False))
        self.spread1(c, p2)

    def gather(self, s, c):
        g = s - self.top
        p1, n1, p2, n2 = self.p1, self.n1, self.p2, self.n2
        if 1 <= g < n2:
            @when(p2 >= g)
            def _():
                self.arrive(self.res.at[c, p1, p2 - g], self.g2.at[c, p2 - g])
                when(p2 < n2 - 1)(lambda: self.gsend2(c, p2 - g, True))
                self.spread1(c, p2 - g)

            @when(p2 + g < n2)
            def _():
                self.arrive(self.res.at[c, p1, p2 + g], self.g2.at[c, p2 + g])
                when(p2 > 0)(lambda: self.gsend2(c, p2 + g, False))
                self.spread1(c, p2 + g)

        for h in range(n2):
            k = g - h
            if not 1 <= k < n1:
                continue
            for side in ((-1, 1) if h else (1,)):
                q2 = p2 + side * h

                @when(q2 >= 0 if side < 0 else q2 < n2)
                def _():
                    @when(p1 >= k)
                    def _():
                        self.arrive(self.res.at[c, p1 - k, q2], self.g1.at[c, p1 - k, q2])
                        when(p1 < n1 - 1)(lambda: self.gsend1(c, p1 - k, q2, True))

                    @when(p1 + k < n1)
                    def _():
                        self.arrive(self.res.at[c, p1 + k, q2], self.g1.at[c, p1 + k, q2])
                        when(p1 > 0)(lambda: self.gsend1(c, p1 + k, q2, False))


def exchange_kernel(dims, frag, inner, snapshot, momentum, bits, inner_v, res_a, res_b, mom_next, *scratch):
    outer, inner_n, chunks, share, wide = dims
    replicas = outer * inner_n
    frags = inner_v.shape[0]
    bbuf, snap, mom, acc_a, acc_b, wsem, bsem, ssem, msem = scratch[:9]
    bufs_a, bufs_b = (*scratch[9:14], res_a), (*scratch[14:19], res_b)
    sems_a, sems_b = scratch[19:31], scratch[31:43]
    me = lax.axis_index("replica")
    y, z = lax.rem(me, inner_n), lax.div(me, inner_n)
    line_y, line_z = (y, inner_n, 1), (z, outer, inner_n)

    def parts_at(r, draining):
        at_y, at_z = (r % inner_n, inner_n, 1), (r // inner_n, outer, inner_n)
        return (
            Part(bufs_a, sems_a, at_y, at_z, r, 0, wide, draining),
            Part(bufs_b, sems_b, at_z, at_y, r, wide, share - wide, draining),
        )

    def loads(c, slot):
        return (
            pltpu.make_async_copy(inner.at[0, :, c], inner_v.at[:, c], wsem.at[c]),
            pltpu.make_async_copy(bits.at[c], bbuf.at[slot], bsem.at[slot]),
            pltpu.make_async_copy(snapshot.at[c], snap.at[c], ssem.at[c]),
        )

    for copy in loads(0, 0):
        copy.start()
    mom_copy = pltpu.make_async_copy(momentum, mom, msem)
    mom_copy.start()

    barrier = pltpu.get_barrier_semaphore()
    count = 0
    for pos, n, step in (line_y, line_z):
        for delta, there in ((-step, pos > 0), (step, pos < n - 1)):
            @pl.when(there)
            def _():
                pl.semaphore_signal(barrier, inc=1, device_id={"replica": me + delta}, device_id_type=MESH)

            count = count + there.astype(jnp.int32)
    pl.semaphore_wait(barrier, count)
    mom_copy.wait()

    def round_chunk(c):
        slot = lax.rem(c, 2)

        @pl.when(c + 1 < chunks)
        def _():
            for copy in loads(c + 1, 1 - slot):
                copy.start()

        for copy in loads(c, slot):
            copy.wait()
        which = frag[0]
        for b in range(replicas):
            cols = slice(b * share, (b + 1) * share)
            chosen = inner_v[0, c, :, cols].astype(jnp.float32)
            for f in range(1, frags):
                chosen = jnp.where(which == f, inner_v[f, c, :, cols].astype(jnp.float32), chosen)
            scaled = grid_scale * (snap[c, :, cols].astype(jnp.float32) - chosen)
            lower = jnp.floor(scaled)
            raised = jnp.where(bbuf[slot, :, cols].astype(jnp.float32) < bit_levels * (scaled - lower), 1.0, 0.0)
            rounded = ((lower + raised) / grid_scale).astype(jnp.bfloat16)
            bz, by = b // inner_n, b % inner_n
            bufs_a[0][c, by, bz] = rounded[:, :wide]
            bufs_b[0][c, bz, by] = rounded[:, wide:]

    def stage(s, c, part):
        part.hop1(s, c)
        part.hop2(s, c)
        if s == top:
            part.update(c, snap, mom, mom_next, acc_b if part.cols else acc_a, replicas, share)
        part.gather(s, c)

    top = inner_n + outer - 2
    stages = 2 * top + 1

    def at_my_place(todo, draining):
        for r in range(replicas):
            pl.when(me == r)(functools.partial(todo, parts_at(r, draining)))

    plan = order_of(stages)
    split = plan.index((-1, 0, 0))

    def tick(t, carry):
        def run(entries, parts):
            for s, which_part, lag in entries:
                c = t - lag

                @pl.when(jnp.logical_and(c >= 0, c < chunks))
                def _():
                    stage(s, c, parts[which_part])

        at_my_place(functools.partial(run, plan[:split]), False)
        pl.when(t < chunks)(functools.partial(round_chunk, t))
        at_my_place(functools.partial(run, plan[split + 1:]), False)
        return carry

    lax.fori_loop(0, chunks + max(lag for _, _, lag in plan), tick, 0)

    def drain_at(parts):
        def drain(c, carry):
            for s in range(stages):
                for part in parts:
                    stage(s, c, part)
            return carry

        lax.fori_loop(0, chunks, drain, 0)

    at_my_place(drain_at, True)


def finish_kernel(frag, inner_v, res_a, res_b, mom_next, snap_out, mom_out, inner_out, snap_v, blend_v, mom_sem, pass_sem, snap_sem, blend_sem):
    frags, chunks = inner_v.shape[:2]
    n_y, n_z = res_a.shape[1], res_a.shape[2]
    wide = res_a.shape[4]
    share = wide + res_b.shape[4]
    which = frag[0]
    waits = [pltpu.make_async_copy(mom_next, mom_out, mom_sem)]
    for j in range(1, frags):
        other = lax.rem(which + j, frags)
        waits.append(pltpu.make_async_copy(inner_v.at[other], inner_out.at[0, other], pass_sem.at[j]))

    def puts(c):
        return (
            pltpu.make_async_copy(snap_v.at[c], snap_out.at[c], snap_sem.at[c]),
            pltpu.make_async_copy(blend_v.at[c], inner_out.at[0, which, c], blend_sem.at[c]),
        )

    for copy in waits:
        copy.start()

    def blend(c, carry):
        for bz in range(n_z):
            for by in range(n_y):
                first = (bz * n_y + by) * share
                for col, part in ((first, res_a[c, by, bz]), (first + wide, res_b[c, bz, by])):
                    cols = slice(col, col + part.shape[1])
                    snap_v[c, :, cols] = part
                    blend_v[c, :, cols] = (
                        blend_keep * inner_v[which, c, :, cols].astype(jnp.float32)
                        + (1.0 - blend_keep) * part.astype(jnp.float32)
                    ).astype(jnp.bfloat16)
        for copy in puts(c):
            copy.start()
        return carry

    lax.fori_loop(0, chunks, blend, 0)
    for copy in waits:
        copy.wait()

    def settle(c, carry):
        for copy in puts(c):
            copy.wait()
        return carry

    lax.fori_loop(0, chunks, settle, 0)


def body(inner_weights, snapshot, momentum, rand_bits, fragment):
    n = lax.axis_size("replica")
    outer, inner_n = grid_of(n)
    frags, rows, width = inner_weights.shape[1:]
    share = momentum.shape[1]
    wide = max(1, min(share // 128 - 1, round(0.6 * share / 128))) * 128
    narrow = share - wide
    chunks = rows // CHUNK_ROWS
    bf, f32 = jnp.bfloat16, jnp.float32
    dma = pltpu.SemaphoreType.DMA

    def bufs(n1, n2, w):
        full = (chunks, n1, n2, CHUNK_ROWS, w)
        line = (chunks, n2, CHUNK_ROWS, w)
        return [pltpu.VMEM(s, bf) for s in (full, full, full, line, line)]

    def sems(n1, n2):
        one, two, both = (chunks, n1), (chunks, n2), (chunks, n1, n2)
        return [dma(s) for s in (one,) * 3 + (two,) * 6 + (both,) * 3]

    scratch = [
        pltpu.VMEM((2, CHUNK_ROWS, width), jnp.int32),
        pltpu.VMEM((chunks, CHUNK_ROWS, width), bf),
        pltpu.VMEM((chunks, CHUNK_ROWS, share), f32),
        pltpu.VMEM((CHUNK_ROWS, wide), f32),
        pltpu.VMEM((CHUNK_ROWS, narrow), f32),
        dma((chunks,)), dma((2,)), dma((chunks,)), dma,
        *bufs(inner_n, outer, wide), *bufs(outer, inner_n, narrow),
        *sems(inner_n, outer), *sems(outer, inner_n),
    ]
    anywhere = pl.BlockSpec(memory_space=pl.ANY)
    in_vmem = pl.BlockSpec(memory_space=pltpu.VMEM)
    in_smem = pl.BlockSpec(memory_space=pltpu.SMEM)
    held = pl.pallas_call(
        functools.partial(exchange_kernel, (outer, inner_n, chunks, share, wide)),
        out_shape=(
            pltpu.VMEM((frags, chunks, CHUNK_ROWS, width), bf),
            pltpu.VMEM((chunks, inner_n, outer, CHUNK_ROWS, wide), bf),
            pltpu.VMEM((chunks, outer, inner_n, CHUNK_ROWS, narrow), bf),
            pltpu.VMEM((chunks, CHUNK_ROWS, share), f32),
        ),
        in_specs=[in_smem] + [pl.BlockSpec(memory_space=pltpu.HBM)] * 4,
        out_specs=(in_vmem,) * 4,
        scratch_shapes=scratch,
        compiler_params=pltpu.CompilerParams(
            collective_id=0, has_side_effects=True, vmem_limit_bytes=EXCHANGE_VMEM
        ),
        name="exchange",
    )(
        fragment,
        inner_weights.reshape(1, frags, chunks, CHUNK_ROWS, width),
        snapshot.reshape(chunks, CHUNK_ROWS, width),
        momentum.reshape(chunks, CHUNK_ROWS, share),
        rand_bits.reshape(chunks, CHUNK_ROWS, width),
    )

    new_snapshot, new_momentum, new_inner = pl.pallas_call(
        finish_kernel,
        in_specs=[in_smem] + [in_vmem] * 4,
        out_specs=(anywhere,) * 3,
        out_shape=(
            jax.ShapeDtypeStruct((chunks, CHUNK_ROWS, width), bf),
            jax.ShapeDtypeStruct((chunks, CHUNK_ROWS, share), f32),
            jax.ShapeDtypeStruct((1, frags, chunks, CHUNK_ROWS, width), bf),
        ),
        scratch_shapes=[
            pltpu.VMEM((chunks, CHUNK_ROWS, width), bf),
            pltpu.VMEM((chunks, CHUNK_ROWS, width), bf),
            dma, dma((frags,)), dma((chunks,)), dma((chunks,)),
        ],
        compiler_params=pltpu.CompilerParams(vmem_limit_bytes=FINISH_VMEM),
        name="finish",
    )(fragment, *held)
    return new_snapshot.reshape(rows, width), new_momentum.reshape(rows, share), new_inner.reshape(inner_weights.shape)


def solution(mesh):
    placed = (
        P("replica", None, "fsdp", None),
        P("fsdp", None),
        P("fsdp", "replica"),
        P("replica", "fsdp", None),
        P(),
    )
    return jax.shard_map(
        body,
        mesh=mesh,
        in_specs=placed,
        out_specs=(P("fsdp", None), P("fsdp", "replica"), P("replica", None, "fsdp", None)),
        check_vma=False,
    )
```

```python
import functools
import itertools

import jax
import jax.numpy as jnp
from jax import lax
from jax.experimental import pallas as pl
from jax.experimental.pallas import tpu as pltpu
from jax.sharding import PartitionSpec as P

momentum_coef = 0.9
outer_rate = 0.7
blend_keep = 0.5
grid_scale = 4.0
bit_levels = 4096.0
MESH = pl.DeviceIdType.MESH
CHUNK_ROWS = 32
TUNED = [
    (0, 3, 0, 12), (0, 0, 0, 3), (0, 4, 1, 11), (0, 2, 1, 6), (1, 6, 0, 62),
    (0, 5, 1, 20), (1, 4, 1, 11), (0, 1, 1, 4), (0, 6, 0, 24), (1, 4, 0, 11),
    (0, 2, 0, 10), (0, 8, 0, 78), (1, 3, 1, 9), (0, 4, 0, 16), (1, 3, 0, 10),
    (0, 7, 1, 33), (0, 7, 0, 26), (-1, -1, 0, 0), (1, 2, 1, 7), (1, 5, 0, 14),
    (0, 1, 0, 7), (1, 1, 1, 6), (1, 0, 1, 2), (0, 8, 1, 79), (1, 1, 0, 4),
    (1, 6, 1, 67), (0, 5, 0, 21), (1, 5, 1, 12), (0, 6, 1, 26), (1, 2, 0, 8),
    (0, 3, 1, 9), (1, 0, 0, 1), (0, 0, 1, 0),
]
EXCHANGE_VMEM = 42 << 20
FINISH_VMEM = 10 << 20


def grid_of(n):
    inner = max(k for k in range(1, n + 1) if n % k == 0 and k * k <= n)
    return n // inner, inner


def owners(n):
    ends = n // 4
    return ([*range(ends), *range(n - (n // 2 - ends), n)], [*range(ends, ends + n // 2)])


def depth(n, group):
    return max(max(q, n - 1 - q) for q in group)


def stages_of(n_y, n_z, kind):
    return 2 * (n_y - 1) + 2 * depth(n_z, owners(n_z)[kind]) + 1


def order_of(n_y, n_z):
    counts = [stages_of(n_y, n_z, kind) for kind in (0, 1)]
    if counts == [max(s for k, s, _, _ in TUNED if k == kind) + 1 for kind in (0, 1)]:
        return TUNED
    order = []
    for s in range(max(counts) - 1, 0, -1):
        order += [(kind, s, part, s) for kind in (0, 1) if s < counts[kind] for part in (0, 1)]
    return [*order, (-1, -1, 0, 0), *((kind, 0, part, 0) for kind in (0, 1) for part in (0, 1))]


class Line:
    def __init__(self, pos, n, step, me):
        self.pos, self.n, self.step, self.me = pos, n, step, me

    def send(self, src, dst, send_sem, recv_sem, right):
        copy = pltpu.make_async_remote_copy(
            src_ref=src, dst_ref=dst, send_sem=send_sem, recv_sem=recv_sem,
            device_id={"replica": self.me + (self.step if right else -self.step)}, device_id_type=MESH,
        )
        copy.start()

    def settle(self, ref, sem):
        return pltpu.make_async_remote_copy(
            src_ref=ref, dst_ref=ref, send_sem=sem, recv_sem=sem,
            device_id={"replica": self.me}, device_id_type=MESH,
        )

    def arrive(self, dst, recv_sem):
        self.settle(dst, recv_sem).wait_recv()

    def reduce(self, h, group, i, block, arrived, from_left, from_right, sems, add):
        send_sem, left_sem, right_sem = sems
        p, n = self.pos, self.n
        for slot, q in sorted(enumerate(group), key=lambda e: -e[1]):
            if p == h and p <= q and (h > 0 or q > 0):
                if p > 0:
                    self.arrive(from_left.at[i, slot], left_sem.at[i, slot])
                    if p < q or arrived:
                        add(block(slot), from_left.at[i, slot])
                if p < q:
                    self.send(block(slot), from_left.at[i, slot], send_sem, left_sem.at[i, slot], True)
        for slot, q in enumerate(group):
            if p == n - 1 - h and p >= q and (h > 0 or q < n - 1):
                if p < n - 1:
                    self.arrive(from_right.at[i, slot], right_sem.at[i, slot])
                    if p > q or arrived:
                        add(block(slot), from_right.at[i, slot])
                if p > q:
                    self.send(block(slot), from_right.at[i, slot], send_sem, right_sem.at[i, slot], False)

    def spread(self, k, group, i, block, sems):
        recv_sem, right_sem, left_sem = sems
        p, n = self.pos, self.n
        for slot, q in enumerate(group):
            here = block(slot)
            if k == 0 and p != q or k > 0 and abs(p - q) != k:
                continue
            if k > 0:
                self.arrive(here, recv_sem.at[i, slot])
            if p < n - 1 and p >= q:
                self.send(here, here, right_sem, recv_sem.at[i, slot], True)
            if p > 0 and p <= q:
                self.send(here, here, left_sem, recv_sem.at[i, slot], False)


class Part:
    def __init__(self, refs, sems, line_y, line_z, ctx, y_first):
        self.own, self.yr, self.yl, self.zr, self.zl, self.res = refs
        self.sy, self.sz, self.gy, self.gz = (sems[j : j + 3] for j in (0, 3, 6, 9))
        self.line_y, self.line_z, self.y_first = line_y, line_z, y_first
        self.ctx = ctx

    def add(self, block, recv):
        block[...] = block[...] + recv[...]

    def update(self, i, rc, slot):
        snap, mom, mom_next, acc, replicas, share, cols, width = self.ctx
        y, z = self.line_y.pos, self.line_z.pos
        line, block = (self.line_z, slot) if self.y_first else (self.line_y, y)
        left, right = (self.zr, self.zl) if self.y_first else (self.yr, self.yl)
        here = (i, y, slot) if self.y_first else (i, slot, y)
        acc[...] = self.own[here].astype(jnp.float32)
        if line.pos > 0:
            acc[...] += left[i, block].astype(jnp.float32)
        if line.pos < line.n - 1:
            acc[...] += right[i, block].astype(jnp.float32)
        start = (z * self.line_y.n + y) * share + cols
        strip = pl.ds(cols, width)
        grad = acc[...] / replicas
        moment = momentum_coef * mom[rc, :, strip] + grad
        mom_next[rc, :, strip] = moment
        base = snap[rc, :, pl.ds(start, width)].astype(jnp.float32)
        self.res[here] = (base - outer_rate * (grad + momentum_coef * moment)).astype(jnp.bfloat16)

    def stage(self, s, i, rc, kind):
        line_y, line_z = self.line_y, self.line_z
        y, z, last_y = line_y.pos, line_z.pos, line_y.n - 1
        rows, group = [*range(line_y.n)], owners(line_z.n)[kind]
        sent, *landed = self.sz
        on_z = (sent.at[kind], *landed)
        sent, *landed = self.sy
        on_y = (sent.at[0], *landed)
        landed, right, left = self.gz
        out_z = (landed, right.at[kind], left.at[kind])
        landed, right, left = self.gy
        out_y = (landed, right.at[0], left.at[0])
        far = depth(line_z.n, group)
        slot = group.index(z) if z in group else None
        if self.y_first:
            if s <= last_y:
                line_y.reduce(s, rows, i, lambda q: self.own.at[i, q], True, self.yr, self.yl, on_y, self.add)
            h = s - last_y
            if 0 <= h <= far:
                line_z.reduce(h, group, i, lambda q: self.own.at[i, y, q], False, self.zr, self.zl, on_z, self.add)
            if h == far and slot is not None:
                self.update(i, rc, slot)
            if 0 <= h - far <= far:
                line_z.spread(h - far, group, i, lambda q: self.res.at[i, y, q], out_z)
            if 0 <= h - 2 * far <= last_y:
                line_y.spread(h - 2 * far, rows, i, lambda q: self.res.at[i, q], out_y)
        else:
            if s <= far:
                line_z.reduce(s, group, i, lambda q: self.own.at[i, q], True, self.zr, self.zl, on_z, self.add)
            h = s - far
            if slot is not None and 0 <= h <= last_y:
                line_y.reduce(h, rows, i, lambda q: self.own.at[i, slot, q], False, self.yr, self.yl, on_y, self.add)
            if slot is not None and h == last_y:
                self.update(i, rc, slot)
            if slot is not None and 0 <= h - last_y <= last_y:
                line_y.spread(h - last_y, rows, i, lambda q: self.res.at[i, slot, q], out_y)
            k = h - 2 * last_y
            if 0 <= k <= far:
                line_z.spread(k, group, i, lambda q: self.res.at[i, q], out_z)


    def settle(self, chunks):
        line_y, line_z = self.line_y, self.line_z
        y, z = line_y.pos, line_z.pos
        waits = []

        def on_y(ref, count, sem):
            waits.append((ref.at[:, :count] if self.y_first else ref.at[:chunks, 0, :count], sem.at[0], count))

        def on_z(ref, count, sem, kind):
            waits.append((ref.at[:chunks, 0, :count] if self.y_first else ref.at[:chunks, :count], sem.at[kind], count))

        on_y(self.own, line_y.n - 1, self.sy[0])
        on_y(self.res, (y + 1) * (y < line_y.n - 1), self.gy[1])
        on_y(self.res, (line_y.n - y) * (y > 0), self.gy[2])
        for kind, group in enumerate(owners(line_z.n)):
            on_z(self.own, sum(q != z for q in group), self.sz[0], kind)
            on_z(self.res, sum(q <= z for q in group) * (z < line_z.n - 1), self.gz[1], kind)
            on_z(self.res, sum(q >= z for q in group) * (z > 0), self.gz[2], kind)
        for ref, sem, count in waits:
            if count:
                line_y.settle(ref, sem).wait_send()


def exchange_kernel(dims, frag, inner, snapshot, momentum, bits, inner_v, res_a, res_b, mom_next, *scratch):
    n_z, n_y, chunks, share, wide = dims
    replicas, total = n_z * n_y, 2 * chunks
    frags = inner_v.shape[0]
    bbuf, snap, mom, acc_a, acc_b, wsem, bsem, ssem, msem = scratch[:9]
    refs_a, refs_b = (*scratch[9:14], res_a), (*scratch[14:19], res_b)
    sems_a, sems_b = scratch[19:31], scratch[31:43]
    me = lax.axis_index("replica")
    y, z = lax.rem(me, n_y), lax.div(me, n_y)
    groups = owners(n_z)
    strip = n_y * share

    def parts_at(r):
        line_y = Line(r % n_y, n_y, 1, r)
        line_z = Line(r // n_y, n_z, n_y, r)
        ctx = (snap, mom, mom_next)
        return (
            Part(refs_a, sems_a, line_y, line_z, (*ctx, acc_a, replicas, share, 0, wide), True),
            Part(refs_b, sems_b, line_y, line_z, (*ctx, acc_b, replicas, share, wide, share - wide), False),
        )

    def loads(rc, kind):
        i = 2 * rc + kind
        copies = []
        for slot, owner in enumerate(groups[kind]):
            cols = slice(owner * strip, (owner + 1) * strip)
            copies += [
                pltpu.make_async_copy(inner.at[0, :, rc, :, cols], inner_v.at[:, rc, :, cols], wsem.at[i, slot]),
                pltpu.make_async_copy(bits.at[rc, :, cols], bbuf.at[kind, slot], bsem.at[kind, slot]),
                pltpu.make_async_copy(snapshot.at[rc, :, cols], snap.at[rc, :, cols], ssem.at[i, slot]),
            ]
        return copies

    for copy in loads(0, 0):
        copy.start()
    mom_copy = pltpu.make_async_copy(momentum, mom, msem)
    mom_copy.start()

    barrier = pltpu.get_barrier_semaphore()
    count = 0
    for pos, n, step in ((y, n_y, 1), (z, n_z, n_y)):
        for delta, there in ((-step, pos > 0), (step, pos < n - 1)):
            @pl.when(there)
            def _():
                pl.semaphore_signal(barrier, inc=1, device_id={"replica": me + delta}, device_id_type=MESH)

            count = count + there.astype(jnp.int32)

    def round_chunk(rc, kind):
        @pl.when(rc + kind < chunks)
        def _():
            for copy in loads(rc + kind, 1 - kind):
                copy.start()

        for copy in loads(rc, kind):
            copy.wait()
        which = frag[0]
        i = 2 * rc + kind
        for slot, owner in enumerate(groups[kind]):
            for by in range(n_y):
                cols = slice(owner * strip + by * share, owner * strip + (by + 1) * share)
                chosen = inner_v[0, rc, :, cols]
                for f in range(1, frags):
                    chosen = jnp.where(which == f, inner_v[f, rc, :, cols], chosen)
                scaled = grid_scale * (snap[rc, :, cols].astype(jnp.float32) - chosen.astype(jnp.float32))
                lower = jnp.floor(scaled)
                drawn = bbuf[kind, slot, :, by * share : (by + 1) * share].astype(jnp.float32)
                raised = jnp.where(drawn < bit_levels * (scaled - lower), 1.0, 0.0)
                rounded = ((lower + raised) / grid_scale).astype(jnp.bfloat16)
                refs_a[0][i, by, slot] = rounded[:, :wide]
                refs_b[0][i, slot, by] = rounded[:, wide:]

    plan = order_of(n_y, n_z)
    split = [kind for kind, _, _, _ in plan].index(-1)
    last = max(lag for _, _, _, lag in plan)

    def at_my_place(todo):
        for r in range(replicas):
            pl.when(me == r)(functools.partial(todo, parts_at(r)))

    def entries_of(parity, entries):
        for kind, s, part, lag in entries:
            if (parity - lag - kind) % 2 == 0:
                yield (parity - lag - kind) // 2, kind, s, part

    def two_ticks(u, carry):
        def run(entries, parts):
            for ahead, some in itertools.groupby(entries, key=lambda e: e[0]):
                rc = u + ahead

                @pl.when(jnp.logical_and(rc >= 0, rc < chunks))
                def _():
                    for _, kind, s, part in some:
                        parts[part].stage(s, 2 * rc + kind, rc, kind)

        before, after = ([[*entries_of(parity, p)] for parity in (0, 1)] for p in (plan[:split], plan[split + 1 :]))
        at_my_place(functools.partial(run, before[0]))
        pl.when(u < chunks)(functools.partial(round_chunk, u, 1))
        at_my_place(functools.partial(run, after[0] + before[1]))
        pl.when(u + 1 < chunks)(functools.partial(round_chunk, u + 1, 0))
        at_my_place(functools.partial(run, after[1]))
        return carry

    round_chunk(0, 0)
    pl.semaphore_wait(barrier, count)
    mom_copy.wait()
    lax.fori_loop(0, pl.cdiv(total + last, 2), two_ticks, 0)

    def settle(parts):
        for part in parts:
            part.settle(chunks)

    at_my_place(settle)


def finish_kernel(frag, inner_v, res_a, res_b, mom_next, snap_out, mom_out, inner_out, snap_v, blend_v, mom_sem, pass_sem, snap_sem, blend_sem):
    frags, chunks = inner_v.shape[:2]
    n_y, n_z = res_a.shape[1], 2 * res_a.shape[2]
    wide = res_a.shape[4]
    share = wide + res_b.shape[4]
    which = frag[0]
    waits = [pltpu.make_async_copy(mom_next, mom_out, mom_sem)]
    for j in range(1, frags):
        other = lax.rem(which + j, frags)
        waits.append(pltpu.make_async_copy(inner_v.at[other], inner_out.at[0, other], pass_sem.at[j]))

    def puts(c):
        return (
            pltpu.make_async_copy(snap_v.at[c], snap_out.at[c], snap_sem.at[c]),
            pltpu.make_async_copy(blend_v.at[c], inner_out.at[0, which, c], blend_sem.at[c]),
        )

    for copy in waits:
        copy.start()

    def blend(c, carry):
        for kind, group in enumerate(owners(n_z)):
            i = 2 * c + kind
            for slot, by in ((slot, by) for slot in range(len(group)) for by in range(n_y)):
                first = (group[slot] * n_y + by) * share
                for col, part in ((first, res_a[i, by, slot]), (first + wide, res_b[i, slot, by])):
                    cols = slice(col, col + part.shape[1])
                    snap_v[c, :, cols] = part
                    blend_v[c, :, cols] = (
                        blend_keep * inner_v[which, c, :, cols].astype(jnp.float32)
                        + (1.0 - blend_keep) * part.astype(jnp.float32)
                    ).astype(jnp.bfloat16)
        for copy in puts(c):
            copy.start()
        return carry

    lax.fori_loop(0, chunks, blend, 0)
    for copy in waits:
        copy.wait()

    def settle(c, carry):
        for copy in puts(c):
            copy.wait()
        return carry

    lax.fori_loop(0, chunks, settle, 0)


def body(inner_weights, snapshot, momentum, rand_bits, fragment):
    n = lax.axis_size("replica")
    outer, inner_n = grid_of(n)
    frags, rows, width = inner_weights.shape[1:]
    share = momentum.shape[1]
    wide = max(1, min(share // 128 - 1, round(0.6 * share / 128))) * 128
    narrow = share - wide
    chunks = rows // CHUNK_ROWS
    bf, f32 = jnp.bfloat16, jnp.float32
    dma = pltpu.SemaphoreType.DMA

    half, total = outer // 2, 2 * chunks

    def bufs(w, y_first):
        block = (CHUNK_ROWS, w)
        own = (total, inner_n, half, *block) if y_first else (total, half, inner_n, *block)
        line_y = own if y_first else (total, inner_n, *block)
        line_z = (total, half, *block) if y_first else own
        return [pltpu.VMEM(s, bf) for s in (own, line_y, line_y, line_z, line_z)]

    def sems():
        on_y, on_z = (total, inner_n), (total, half)
        one, two = (1,), (2,)
        return [dma(s) for s in (one, on_y, on_y, two, on_z, on_z, on_y, one, one, on_z, two, two)]

    scratch = [
        pltpu.VMEM((2, half, CHUNK_ROWS, inner_n * share), jnp.int32),
        pltpu.VMEM((chunks, CHUNK_ROWS, width), bf),
        pltpu.VMEM((chunks, CHUNK_ROWS, share), f32),
        pltpu.VMEM((CHUNK_ROWS, wide), f32),
        pltpu.VMEM((CHUNK_ROWS, narrow), f32),
        dma((total, half)), dma((2, half)), dma((total, half)), dma,
        *bufs(wide, True), *bufs(narrow, False),
        *sems(), *sems(),
    ]
    anywhere = pl.BlockSpec(memory_space=pl.ANY)
    in_vmem = pl.BlockSpec(memory_space=pltpu.VMEM)
    in_smem = pl.BlockSpec(memory_space=pltpu.SMEM)
    held = pl.pallas_call(
        functools.partial(exchange_kernel, (outer, inner_n, chunks, share, wide)),
        out_shape=(
            pltpu.VMEM((frags, chunks, CHUNK_ROWS, width), bf),
            pltpu.VMEM((total, inner_n, half, CHUNK_ROWS, wide), bf),
            pltpu.VMEM((total, half, inner_n, CHUNK_ROWS, narrow), bf),
            pltpu.VMEM((chunks, CHUNK_ROWS, share), f32),
        ),
        in_specs=[in_smem] + [pl.BlockSpec(memory_space=pltpu.HBM)] * 4,
        out_specs=(in_vmem,) * 4,
        scratch_shapes=scratch,
        compiler_params=pltpu.CompilerParams(
            collective_id=0, has_side_effects=True, vmem_limit_bytes=EXCHANGE_VMEM
        ),
        name="exchange",
    )(
        fragment,
        inner_weights.reshape(1, frags, chunks, CHUNK_ROWS, width),
        snapshot.reshape(chunks, CHUNK_ROWS, width),
        momentum.reshape(chunks, CHUNK_ROWS, share),
        rand_bits.reshape(chunks, CHUNK_ROWS, width),
    )

    new_snapshot, new_momentum, new_inner = pl.pallas_call(
        finish_kernel,
        in_specs=[in_smem] + [in_vmem] * 4,
        out_specs=(anywhere,) * 3,
        out_shape=(
            jax.ShapeDtypeStruct((chunks, CHUNK_ROWS, width), bf),
            jax.ShapeDtypeStruct((chunks, CHUNK_ROWS, share), f32),
            jax.ShapeDtypeStruct((1, frags, chunks, CHUNK_ROWS, width), bf),
        ),
        scratch_shapes=[
            pltpu.VMEM((chunks, CHUNK_ROWS, width), bf),
            pltpu.VMEM((chunks, CHUNK_ROWS, width), bf),
            dma, dma((frags,)), dma((chunks,)), dma((chunks,)),
        ],
        compiler_params=pltpu.CompilerParams(vmem_limit_bytes=FINISH_VMEM),
        name="finish",
    )(fragment, *held)
    return new_snapshot.reshape(rows, width), new_momentum.reshape(rows, share), new_inner.reshape(inner_weights.shape)


def solution(mesh):
    placed = (
        P("replica", None, "fsdp", None),
        P("fsdp", None),
        P("fsdp", "replica"),
        P("replica", "fsdp", None),
        P(),
    )
    return jax.shard_map(
        body,
        mesh=mesh,
        in_specs=placed,
        out_specs=(P("fsdp", None), P("fsdp", "replica"), P("replica", None, "fsdp", None)),
        check_vma=False,
    )
```

```python
import functools
import itertools

import jax
import jax.numpy as jnp
from jax import lax
from jax.experimental import pallas as pl
from jax.experimental.pallas import tpu as pltpu
from jax.sharding import PartitionSpec as P

momentum_coef = 0.9
outer_rate = 0.7
blend_keep = 0.5
grid_scale = 4.0
bit_levels = 4096.0
MESH = pl.DeviceIdType.MESH
CHUNK_ROWS = 32
TUNED = [
    (0, 1, 0, 7), (0, 0, 1, 1), (1, 0, 0, 1), (0, 5, 1, 19), (0, 2, 1, 6),
    (1, 6, 0, 22), (0, 2, 0, 10), (1, 6, 1, 32), (1, 4, 1, 10), (1, 0, 1, 2),
    (0, 8, 0, 35), (1, 1, 1, 6), (0, 7, 1, 32), (1, 4, 0, 10), (-1, -1, 0, 0),
    (0, 5, 0, 22), (1, 5, 1, 11), (0, 4, 0, 17), (0, 4, 1, 11), (0, 1, 1, 4),
    (1, 3, 0, 8), (0, 6, 1, 27), (0, 7, 0, 28), (1, 3, 1, 8), (0, 3, 0, 11),
    (0, 3, 1, 7), (1, 2, 1, 7), (0, 0, 0, 4), (1, 2, 0, 6), (0, 8, 1, 35),
    (1, 1, 0, 3), (0, 6, 0, 25), (1, 5, 0, 11),
]
EXCHANGE_VMEM = 42 << 20
FINISH_VMEM = 10 << 20


def grid_of(n):
    inner = max(k for k in range(1, n + 1) if n % k == 0 and k * k <= n)
    return n // inner, inner


def owners(n):
    ends = n // 4
    return ([*range(ends), *range(n - (n // 2 - ends), n)], [*range(ends, ends + n // 2)])


def depth(n, group):
    return max(max(q, n - 1 - q) for q in group)


def stages_of(n_y, n_z, kind):
    return 2 * (n_y - 1) + 2 * depth(n_z, owners(n_z)[kind]) + 1


def order_of(n_y, n_z):
    counts = [stages_of(n_y, n_z, kind) for kind in (0, 1)]
    if counts == [max(s for k, s, _, _ in TUNED if k == kind) + 1 for kind in (0, 1)]:
        return TUNED
    order = []
    for s in range(max(counts) - 1, 0, -1):
        order += [(kind, s, part, s) for kind in (0, 1) if s < counts[kind] for part in (0, 1)]
    return [*order, (-1, -1, 0, 0), *((kind, 0, part, 0) for kind in (0, 1) for part in (0, 1))]


class Line:
    def __init__(self, pos, n, step, me):
        self.pos, self.n, self.step, self.me = pos, n, step, me

    def send(self, src, dst, send_sem, recv_sem, right):
        copy = pltpu.make_async_remote_copy(
            src_ref=src, dst_ref=dst, send_sem=send_sem, recv_sem=recv_sem,
            device_id={"replica": self.me + (self.step if right else -self.step)}, device_id_type=MESH,
        )
        copy.start()

    def settle(self, ref, sem):
        return pltpu.make_async_remote_copy(
            src_ref=ref, dst_ref=ref, send_sem=sem, recv_sem=sem,
            device_id={"replica": self.me}, device_id_type=MESH,
        )

    def arrive(self, dst, recv_sem):
        self.settle(dst, recv_sem).wait_recv()

    def reduce(self, h, group, i, block, arrived, from_left, from_right, sems, add):
        send_sem, left_sem, right_sem = sems
        p, n = self.pos, self.n
        for slot, q in sorted(enumerate(group), key=lambda e: -e[1]):
            if p == h and p <= q and (h > 0 or q > 0):
                if p > 0:
                    self.arrive(from_left.at[i, slot], left_sem.at[i, slot])
                    if p < q or arrived:
                        add(block(slot), from_left.at[i, slot])
                if p < q:
                    self.send(block(slot), from_left.at[i, slot], send_sem, left_sem.at[i, slot], True)
        for slot, q in enumerate(group):
            if p == n - 1 - h and p >= q and (h > 0 or q < n - 1):
                if p < n - 1:
                    self.arrive(from_right.at[i, slot], right_sem.at[i, slot])
                    if p > q or arrived:
                        add(block(slot), from_right.at[i, slot])
                if p > q:
                    self.send(block(slot), from_right.at[i, slot], send_sem, right_sem.at[i, slot], False)

    def spread(self, k, group, i, block, sems):
        recv_sem, right_sem, left_sem = sems
        p, n = self.pos, self.n
        for slot, q in enumerate(group):
            here = block(slot)
            if k == 0 and p != q or k > 0 and abs(p - q) != k:
                continue
            if k > 0:
                self.arrive(here, recv_sem.at[i, slot])
            if p < n - 1 and p >= q:
                self.send(here, here, right_sem, recv_sem.at[i, slot], True)
            if p > 0 and p <= q:
                self.send(here, here, left_sem, recv_sem.at[i, slot], False)


class Part:
    def __init__(self, refs, sems, line_y, line_z, ctx, y_first):
        self.own, self.yr, self.yl, self.zr, self.zl, self.res = refs
        self.sy, self.sz, self.gy, self.gz = (sems[j : j + 3] for j in (0, 3, 6, 9))
        self.line_y, self.line_z, self.y_first = line_y, line_z, y_first
        self.ctx = ctx

    def add(self, block, recv):
        block[...] = block[...] + recv[...]

    def update(self, i, rc, slot):
        snap, mom, mom_next, acc, replicas, share, cols, width = self.ctx
        y, z = self.line_y.pos, self.line_z.pos
        line, block = (self.line_z, slot) if self.y_first else (self.line_y, y)
        left, right = (self.zr, self.zl) if self.y_first else (self.yr, self.yl)
        here = (i, y, slot) if self.y_first else (i, slot, y)
        acc[...] = self.own[here].astype(jnp.float32)
        if line.pos > 0:
            acc[...] += left[i, block].astype(jnp.float32)
        if line.pos < line.n - 1:
            acc[...] += right[i, block].astype(jnp.float32)
        start = (z * self.line_y.n + y) * share + cols
        strip = pl.ds(cols, width)
        grad = acc[...] / replicas
        moment = momentum_coef * mom[rc, :, strip] + grad
        mom_next[rc, :, strip] = moment
        base = snap[rc, :, pl.ds(start, width)].astype(jnp.float32)
        self.res[here] = (base - outer_rate * (grad + momentum_coef * moment)).astype(jnp.bfloat16)

    def stage(self, s, i, rc, kind):
        line_y, line_z = self.line_y, self.line_z
        y, z, last_y = line_y.pos, line_z.pos, line_y.n - 1
        rows, group = [*range(line_y.n)], owners(line_z.n)[kind]
        sent, *landed = self.sz
        on_z = (sent.at[kind], *landed)
        sent, *landed = self.sy
        on_y = (sent.at[0], *landed)
        landed, right, left = self.gz
        out_z = (landed, right.at[kind], left.at[kind])
        landed, right, left = self.gy
        out_y = (landed, right.at[0], left.at[0])
        far = depth(line_z.n, group)
        slot = group.index(z) if z in group else None
        if self.y_first:
            if s <= last_y:
                line_y.reduce(s, rows, i, lambda q: self.own.at[i, q], True, self.yr, self.yl, on_y, self.add)
            h = s - last_y
            if 0 <= h <= far:
                line_z.reduce(h, group, i, lambda q: self.own.at[i, y, q], False, self.zr, self.zl, on_z, self.add)
            if h == far and slot is not None:
                self.update(i, rc, slot)
            if 0 <= h - far <= far:
                line_z.spread(h - far, group, i, lambda q: self.res.at[i, y, q], out_z)
            if 0 <= h - 2 * far <= last_y:
                line_y.spread(h - 2 * far, rows, i, lambda q: self.res.at[i, q], out_y)
        else:
            if s <= far:
                line_z.reduce(s, group, i, lambda q: self.own.at[i, q], True, self.zr, self.zl, on_z, self.add)
            h = s - far
            if slot is not None and 0 <= h <= last_y:
                line_y.reduce(h, rows, i, lambda q: self.own.at[i, slot, q], False, self.yr, self.yl, on_y, self.add)
            if slot is not None and h == last_y:
                self.update(i, rc, slot)
            if slot is not None and 0 <= h - last_y <= last_y:
                line_y.spread(h - last_y, rows, i, lambda q: self.res.at[i, slot, q], out_y)
            k = h - 2 * last_y
            if 0 <= k <= far:
                line_z.spread(k, group, i, lambda q: self.res.at[i, q], out_z)


    def settle(self, chunks):
        line_y, line_z = self.line_y, self.line_z
        y, z = line_y.pos, line_z.pos
        waits = []

        def on_y(ref, count, sem):
            waits.append((ref.at[:, :count] if self.y_first else ref.at[:chunks, 0, :count], sem.at[0], count))

        def on_z(ref, count, sem, kind):
            waits.append((ref.at[:chunks, 0, :count] if self.y_first else ref.at[:chunks, :count], sem.at[kind], count))

        on_y(self.own, line_y.n - 1, self.sy[0])
        on_y(self.res, (y + 1) * (y < line_y.n - 1), self.gy[1])
        on_y(self.res, (line_y.n - y) * (y > 0), self.gy[2])
        for kind, group in enumerate(owners(line_z.n)):
            on_z(self.own, sum(q != z for q in group), self.sz[0], kind)
            on_z(self.res, sum(q <= z for q in group) * (z < line_z.n - 1), self.gz[1], kind)
            on_z(self.res, sum(q >= z for q in group) * (z > 0), self.gz[2], kind)
        for ref, sem, count in waits:
            if count:
                line_y.settle(ref, sem).wait_send()


def exchange_kernel(dims, frag, inner, snapshot, momentum, bits, inner_v, res_a, res_b, mom_next, *scratch):
    n_z, n_y, chunks, share, wide = dims
    replicas, total = n_z * n_y, 2 * chunks
    frags = inner_v.shape[0]
    bbuf, snap, mom, acc_a, acc_b, wsem, bsem, ssem, msem = scratch[:9]
    refs_a, refs_b = (*scratch[9:14], res_a), (*scratch[14:19], res_b)
    sems_a, sems_b = scratch[19:31], scratch[31:43]
    me = lax.axis_index("replica")
    y, z = lax.rem(me, n_y), lax.div(me, n_y)
    groups = owners(n_z)
    strip = n_y * share

    def parts_at(r):
        line_y = Line(r % n_y, n_y, 1, r)
        line_z = Line(r // n_y, n_z, n_y, r)
        ctx = (snap, mom, mom_next)
        return (
            Part(refs_a, sems_a, line_y, line_z, (*ctx, acc_a, replicas, share, 0, wide), True),
            Part(refs_b, sems_b, line_y, line_z, (*ctx, acc_b, replicas, share, wide, share - wide), False),
        )

    def loads(rc, kind):
        i = 2 * rc + kind
        copies = []
        for slot, owner in enumerate(groups[kind]):
            cols = slice(owner * strip, (owner + 1) * strip)
            copies += [
                pltpu.make_async_copy(inner.at[0, :, rc, :, cols], inner_v.at[:, rc, :, cols], wsem.at[i, slot]),
                pltpu.make_async_copy(bits.at[rc, :, cols], bbuf.at[kind, slot], bsem.at[kind, slot]),
                pltpu.make_async_copy(snapshot.at[rc, :, cols], snap.at[rc, :, cols], ssem.at[i, slot]),
            ]
        return copies

    for copy in loads(0, 0):
        copy.start()
    mom_copy = pltpu.make_async_copy(momentum, mom, msem)
    mom_copy.start()

    barrier = pltpu.get_barrier_semaphore()
    count = 0
    for pos, n, step in ((y, n_y, 1), (z, n_z, n_y)):
        for delta, there in ((-step, pos > 0), (step, pos < n - 1)):
            @pl.when(there)
            def _():
                pl.semaphore_signal(barrier, inc=1, device_id={"replica": me + delta}, device_id_type=MESH)

            count = count + there.astype(jnp.int32)

    def round_chunk(rc, kind):
        @pl.when(rc + kind < chunks)
        def _():
            for copy in loads(rc + kind, 1 - kind):
                copy.start()

        for copy in loads(rc, kind):
            copy.wait()
        which = frag[0]
        i = 2 * rc + kind
        for slot, owner in enumerate(groups[kind]):
            for by in range(n_y):
                cols = slice(owner * strip + by * share, owner * strip + (by + 1) * share)
                chosen = inner_v[0, rc, :, cols]
                for f in range(1, frags):
                    chosen = jnp.where(which == f, inner_v[f, rc, :, cols], chosen)
                scaled = grid_scale * (snap[rc, :, cols].astype(jnp.float32) - chosen.astype(jnp.float32))
                lower = jnp.floor(scaled)
                drawn = bbuf[kind, slot, :, by * share : (by + 1) * share].astype(jnp.float32)
                raised = jnp.where(drawn < bit_levels * (scaled - lower), 1.0, 0.0)
                rounded = ((lower + raised) / grid_scale).astype(jnp.bfloat16)
                refs_a[0][i, by, slot] = rounded[:, :wide]
                refs_b[0][i, slot, by] = rounded[:, wide:]

    plan = order_of(n_y, n_z)
    split = [kind for kind, _, _, _ in plan].index(-1)
    last = max(lag for _, _, _, lag in plan)
    first = min(lag for kind, s, _, lag in plan if kind >= 0 and s == n_y - 1 + depth(n_z, groups[kind]))

    def at_my_place(todo):
        for r in range(replicas):
            pl.when(me == r)(functools.partial(todo, parts_at(r)))

    def entries_of(parity, entries):
        for kind, s, part, lag in entries:
            if (parity - lag - kind) % 2 == 0:
                yield (parity - lag - kind) // 2, kind, s, part

    def two_ticks(u, carry, parts):
        def run(entries):
            for ahead, some in itertools.groupby(entries, key=lambda e: e[0]):
                rc = u + ahead

                @pl.when(jnp.logical_and(rc >= 0, rc < chunks))
                def _():
                    for _, kind, s, part in some:
                        parts[part].stage(s, 2 * rc + kind, rc, kind)

        pl.when(u == first // 2)(mom_copy.wait)
        before, after = ([[*entries_of(parity, p)] for parity in (0, 1)] for p in (plan[:split], plan[split + 1 :]))
        run(before[0])
        pl.when(u < chunks)(functools.partial(round_chunk, u, 1))
        run(after[0] + before[1])
        pl.when(u + 1 < chunks)(functools.partial(round_chunk, u + 1, 0))
        run(after[1])
        return carry

    round_chunk(0, 0)
    pl.semaphore_wait(barrier, count)
    ticks = pl.cdiv(total + last, 2)

    def all_ticks(parts):
        lax.fori_loop(0, ticks, lambda u, carry: two_ticks(u, carry, parts), 0)

    at_my_place(all_ticks)

    def settle(parts):
        for part in parts:
            part.settle(chunks)

    at_my_place(settle)


def finish_kernel(frag, inner_v, res_a, res_b, mom_next, snap_out, mom_out, inner_out, snap_v, blend_v, mom_sem, pass_sem, snap_sem, blend_sem):
    frags, chunks = inner_v.shape[:2]
    n_y, n_z = res_a.shape[1], 2 * res_a.shape[2]
    wide = res_a.shape[4]
    share = wide + res_b.shape[4]
    which = frag[0]
    waits = [pltpu.make_async_copy(mom_next, mom_out, mom_sem)]
    for j in range(1, frags):
        other = lax.rem(which + j, frags)
        waits.append(pltpu.make_async_copy(inner_v.at[other], inner_out.at[0, other], pass_sem.at[j]))

    def puts(c):
        return (
            pltpu.make_async_copy(snap_v.at[c], snap_out.at[c], snap_sem.at[c]),
            pltpu.make_async_copy(blend_v.at[c], inner_out.at[0, which, c], blend_sem.at[c]),
        )

    for copy in waits:
        copy.start()

    def blend(c, carry):
        for kind, group in enumerate(owners(n_z)):
            i = 2 * c + kind
            for slot, by in ((slot, by) for slot in range(len(group)) for by in range(n_y)):
                first = (group[slot] * n_y + by) * share
                for col, part in ((first, res_a[i, by, slot]), (first + wide, res_b[i, slot, by])):
                    cols = slice(col, col + part.shape[1])
                    snap_v[c, :, cols] = part
                    blend_v[c, :, cols] = (
                        blend_keep * inner_v[which, c, :, cols].astype(jnp.float32)
                        + (1.0 - blend_keep) * part.astype(jnp.float32)
                    ).astype(jnp.bfloat16)
        for copy in puts(c):
            copy.start()
        return carry

    lax.fori_loop(0, chunks, blend, 0)
    for copy in waits:
        copy.wait()

    def settle(c, carry):
        for copy in puts(c):
            copy.wait()
        return carry

    lax.fori_loop(0, chunks, settle, 0)


def body(inner_weights, snapshot, momentum, rand_bits, fragment):
    n = lax.axis_size("replica")
    outer, inner_n = grid_of(n)
    frags, rows, width = inner_weights.shape[1:]
    share = momentum.shape[1]
    wide = max(1, min(share // 128 - 1, round(0.6 * share / 128))) * 128
    narrow = share - wide
    chunks = rows // CHUNK_ROWS
    bf, f32 = jnp.bfloat16, jnp.float32
    dma = pltpu.SemaphoreType.DMA

    half, total = outer // 2, 2 * chunks

    def bufs(w, y_first):
        block = (CHUNK_ROWS, w)
        own = (total, inner_n, half, *block) if y_first else (total, half, inner_n, *block)
        line_y = own if y_first else (total, inner_n, *block)
        line_z = (total, half, *block) if y_first else own
        return [pltpu.VMEM(s, bf) for s in (own, line_y, line_y, line_z, line_z)]

    def sems():
        on_y, on_z = (total, inner_n), (total, half)
        one, two = (1,), (2,)
        return [dma(s) for s in (one, on_y, on_y, two, on_z, on_z, on_y, one, one, on_z, two, two)]

    scratch = [
        pltpu.VMEM((2, half, CHUNK_ROWS, inner_n * share), jnp.int32),
        pltpu.VMEM((chunks, CHUNK_ROWS, width), bf),
        pltpu.VMEM((chunks, CHUNK_ROWS, share), f32),
        pltpu.VMEM((CHUNK_ROWS, wide), f32),
        pltpu.VMEM((CHUNK_ROWS, narrow), f32),
        dma((total, half)), dma((2, half)), dma((total, half)), dma,
        *bufs(wide, True), *bufs(narrow, False),
        *sems(), *sems(),
    ]
    anywhere = pl.BlockSpec(memory_space=pl.ANY)
    in_vmem = pl.BlockSpec(memory_space=pltpu.VMEM)
    in_smem = pl.BlockSpec(memory_space=pltpu.SMEM)
    held = pl.pallas_call(
        functools.partial(exchange_kernel, (outer, inner_n, chunks, share, wide)),
        out_shape=(
            pltpu.VMEM((frags, chunks, CHUNK_ROWS, width), bf),
            pltpu.VMEM((total, inner_n, half, CHUNK_ROWS, wide), bf),
            pltpu.VMEM((total, half, inner_n, CHUNK_ROWS, narrow), bf),
            pltpu.VMEM((chunks, CHUNK_ROWS, share), f32),
        ),
        in_specs=[in_smem] + [pl.BlockSpec(memory_space=pltpu.HBM)] * 4,
        out_specs=(in_vmem,) * 4,
        scratch_shapes=scratch,
        compiler_params=pltpu.CompilerParams(
            collective_id=0, has_side_effects=True, vmem_limit_bytes=EXCHANGE_VMEM
        ),
        name="exchange",
    )(
        fragment,
        inner_weights.reshape(1, frags, chunks, CHUNK_ROWS, width),
        snapshot.reshape(chunks, CHUNK_ROWS, width),
        momentum.reshape(chunks, CHUNK_ROWS, share),
        rand_bits.reshape(chunks, CHUNK_ROWS, width),
    )

    new_snapshot, new_momentum, new_inner = pl.pallas_call(
        finish_kernel,
        in_specs=[in_smem] + [in_vmem] * 4,
        out_specs=(anywhere,) * 3,
        out_shape=(
            jax.ShapeDtypeStruct((chunks, CHUNK_ROWS, width), bf),
            jax.ShapeDtypeStruct((chunks, CHUNK_ROWS, share), f32),
            jax.ShapeDtypeStruct((1, frags, chunks, CHUNK_ROWS, width), bf),
        ),
        scratch_shapes=[
            pltpu.VMEM((chunks, CHUNK_ROWS, width), bf),
            pltpu.VMEM((chunks, CHUNK_ROWS, width), bf),
            dma, dma((frags,)), dma((chunks,)), dma((chunks,)),
        ],
        compiler_params=pltpu.CompilerParams(vmem_limit_bytes=FINISH_VMEM),
        name="finish",
    )(fragment, *held)
    return new_snapshot.reshape(rows, width), new_momentum.reshape(rows, share), new_inner.reshape(inner_weights.shape)


def solution(mesh):
    placed = (
        P("replica", None, "fsdp", None),
        P("fsdp", None),
        P("fsdp", "replica"),
        P("replica", "fsdp", None),
        P(),
    )
    return jax.shard_map(
        body,
        mesh=mesh,
        in_specs=placed,
        out_specs=(P("fsdp", None), P("fsdp", "replica"), P("replica", None, "fsdp", None)),
        check_vma=False,
    )
```

```python
import functools
import itertools

import jax
import jax.numpy as jnp
from jax import lax
from jax.experimental import pallas as pl
from jax.experimental.pallas import tpu as pltpu
from jax.sharding import PartitionSpec as P

momentum_coef = 0.9
outer_rate = 0.7
blend_keep = 0.5
grid_scale = 4.0
bit_levels = 4096.0
MESH = pl.DeviceIdType.MESH
CHUNK_ROWS = 32
TUNED = [
    (0, 1, 0, 7), (0, 0, 1, 1), (1, 0, 0, 1), (0, 5, 1, 19), (0, 2, 1, 6),
    (1, 6, 0, 22), (0, 2, 0, 10), (1, 6, 1, 32), (1, 4, 1, 10), (1, 0, 1, 2),
    (0, 8, 0, 35), (1, 1, 1, 6), (0, 7, 1, 32), (1, 4, 0, 10), (-1, -1, 0, 0),
    (0, 5, 0, 22), (1, 5, 1, 11), (0, 4, 0, 17), (0, 4, 1, 11), (0, 1, 1, 4),
    (1, 3, 0, 8), (0, 6, 1, 27), (0, 7, 0, 28), (1, 3, 1, 8), (0, 3, 0, 11),
    (0, 3, 1, 7), (1, 2, 1, 7), (0, 0, 0, 4), (1, 2, 0, 6), (0, 8, 1, 35),
    (1, 1, 0, 3), (0, 6, 0, 25), (1, 5, 0, 11),
]
EXCHANGE_VMEM = 42 << 20
FINISH_VMEM = 10 << 20


def grid_of(n):
    inner = max(k for k in range(1, n + 1) if n % k == 0 and k * k <= n)
    return n // inner, inner


def owners(n):
    ends = n // 4
    return ([*range(ends), *range(n - (n // 2 - ends), n)], [*range(ends, ends + n // 2)])


def depth(n, group):
    return max(max(q, n - 1 - q) for q in group)


def stages_of(n_y, n_z, kind):
    return 2 * (n_y - 1) + 2 * depth(n_z, owners(n_z)[kind]) + 1


def order_of(n_y, n_z):
    counts = [stages_of(n_y, n_z, kind) for kind in (0, 1)]
    if counts == [max(s for k, s, _, _ in TUNED if k == kind) + 1 for kind in (0, 1)]:
        return TUNED
    order = []
    for s in range(max(counts) - 1, 0, -1):
        order += [(kind, s, part, s) for kind in (0, 1) if s < counts[kind] for part in (0, 1)]
    return [*order, (-1, -1, 0, 0), *((kind, 0, part, 0) for kind in (0, 1) for part in (0, 1))]


class Line:
    def __init__(self, pos, n, step, me):
        self.pos, self.n, self.step, self.me = pos, n, step, me

    def send(self, src, dst, send_sem, recv_sem, right):
        copy = pltpu.make_async_remote_copy(
            src_ref=src, dst_ref=dst, send_sem=send_sem, recv_sem=recv_sem,
            device_id={"replica": self.me + (self.step if right else -self.step)}, device_id_type=MESH,
        )
        copy.start()

    def settle(self, ref, sem):
        return pltpu.make_async_remote_copy(
            src_ref=ref, dst_ref=ref, send_sem=sem, recv_sem=sem,
            device_id={"replica": self.me}, device_id_type=MESH,
        )

    def arrive(self, dst, recv_sem):
        self.settle(dst, recv_sem).wait_recv()

    def reduce(self, h, group, i, block, arrived, from_left, from_right, sems, add):
        send_sem, left_sem, right_sem = sems
        p, n = self.pos, self.n
        for slot, q in sorted(enumerate(group), key=lambda e: -e[1]):
            if p == h and p <= q and (h > 0 or q > 0):
                if p > 0:
                    self.arrive(from_left.at[i, slot], left_sem.at[i, slot])
                    if p < q or arrived:
                        add(block(slot), from_left.at[i, slot])
                if p < q:
                    self.send(block(slot), from_left.at[i, slot], send_sem, left_sem.at[i, slot], True)
        for slot, q in enumerate(group):
            if p == n - 1 - h and p >= q and (h > 0 or q < n - 1):
                if p < n - 1:
                    self.arrive(from_right.at[i, slot], right_sem.at[i, slot])
                    if p > q or arrived:
                        add(block(slot), from_right.at[i, slot])
                if p > q:
                    self.send(block(slot), from_right.at[i, slot], send_sem, right_sem.at[i, slot], False)

    def spread(self, k, group, i, block, sems):
        recv_sem, right_sem, left_sem = sems
        p, n = self.pos, self.n
        for slot, q in enumerate(group):
            here = block(slot)
            if k == 0 and p != q or k > 0 and abs(p - q) != k:
                continue
            if k > 0:
                self.arrive(here, recv_sem.at[i, slot])
            if p < n - 1 and p >= q:
                self.send(here, here, right_sem, recv_sem.at[i, slot], True)
            if p > 0 and p <= q:
                self.send(here, here, left_sem, recv_sem.at[i, slot], False)


class Part:
    def __init__(self, refs, sems, line_y, line_z, ctx, y_first):
        self.own, self.yr, self.yl, self.zr, self.zl, self.res = refs
        self.sy, self.sz, self.gy, self.gz = (sems[j : j + 3] for j in (0, 3, 6, 9))
        self.line_y, self.line_z, self.y_first = line_y, line_z, y_first
        self.ctx = ctx

    def add(self, block, recv):
        block[...] = block[...] + recv[...]

    def update(self, i, rc, slot):
        snap, mom, mom_next, acc, replicas, share, cols, width = self.ctx
        y, z = self.line_y.pos, self.line_z.pos
        line, block = (self.line_z, slot) if self.y_first else (self.line_y, y)
        left, right = (self.zr, self.zl) if self.y_first else (self.yr, self.yl)
        here = (i, y, slot) if self.y_first else (i, slot, y)
        acc[...] = self.own[here].astype(jnp.float32)
        if line.pos > 0:
            acc[...] += left[i, block].astype(jnp.float32)
        if line.pos < line.n - 1:
            acc[...] += right[i, block].astype(jnp.float32)
        start = (z * self.line_y.n + y) * share + cols
        strip = pl.ds(cols, width)
        grad = acc[...] / replicas
        moment = momentum_coef * mom[rc, :, strip] + grad
        mom_next[rc, :, strip] = moment
        base = snap[rc, :, pl.ds(start, width)].astype(jnp.float32)
        self.res[here] = (base - outer_rate * (grad + momentum_coef * moment)).astype(jnp.bfloat16)

    def stage(self, s, i, rc, kind):
        line_y, line_z = self.line_y, self.line_z
        y, z, last_y = line_y.pos, line_z.pos, line_y.n - 1
        rows, group = [*range(line_y.n)], owners(line_z.n)[kind]
        sent, *landed = self.sz
        on_z = (sent.at[kind], *landed)
        sent, *landed = self.sy
        on_y = (sent.at[0], *landed)
        landed, right, left = self.gz
        out_z = (landed, right.at[kind], left.at[kind])
        landed, right, left = self.gy
        out_y = (landed, right.at[0], left.at[0])
        far = depth(line_z.n, group)
        slot = group.index(z) if z in group else None
        if self.y_first:
            if s <= last_y:
                line_y.reduce(s, rows, i, lambda q: self.own.at[i, q], True, self.yr, self.yl, on_y, self.add)
            h = s - last_y
            if 0 <= h <= far:
                line_z.reduce(h, group, i, lambda q: self.own.at[i, y, q], False, self.zr, self.zl, on_z, self.add)
            if h == far and slot is not None:
                self.update(i, rc, slot)
            if 0 <= h - far <= far:
                line_z.spread(h - far, group, i, lambda q: self.res.at[i, y, q], out_z)
            if 0 <= h - 2 * far <= last_y:
                line_y.spread(h - 2 * far, rows, i, lambda q: self.res.at[i, q], out_y)
        else:
            if s <= far:
                line_z.reduce(s, group, i, lambda q: self.own.at[i, q], True, self.zr, self.zl, on_z, self.add)
            h = s - far
            if slot is not None and 0 <= h <= last_y:
                line_y.reduce(h, rows, i, lambda q: self.own.at[i, slot, q], False, self.yr, self.yl, on_y, self.add)
            if slot is not None and h == last_y:
                self.update(i, rc, slot)
            if slot is not None and 0 <= h - last_y <= last_y:
                line_y.spread(h - last_y, rows, i, lambda q: self.res.at[i, slot, q], out_y)
            k = h - 2 * last_y
            if 0 <= k <= far:
                line_z.spread(k, group, i, lambda q: self.res.at[i, q], out_z)


    def settle(self, chunks):
        line_y, line_z = self.line_y, self.line_z
        y, z = line_y.pos, line_z.pos
        waits = []

        def on_y(ref, count, sem):
            waits.append((ref.at[:, :count] if self.y_first else ref.at[:chunks, 0, :count], sem.at[0], count))

        def on_z(ref, count, sem, kind):
            waits.append((ref.at[:chunks, 0, :count] if self.y_first else ref.at[:chunks, :count], sem.at[kind], count))

        on_y(self.own, line_y.n - 1, self.sy[0])
        on_y(self.res, (y + 1) * (y < line_y.n - 1), self.gy[1])
        on_y(self.res, (line_y.n - y) * (y > 0), self.gy[2])
        for kind, group in enumerate(owners(line_z.n)):
            on_z(self.own, sum(q != z for q in group), self.sz[0], kind)
            on_z(self.res, sum(q <= z for q in group) * (z < line_z.n - 1), self.gz[1], kind)
            on_z(self.res, sum(q >= z for q in group) * (z > 0), self.gz[2], kind)
        for ref, sem, count in waits:
            if count:
                line_y.settle(ref, sem).wait_send()


def exchange_kernel(dims, frag, inner, snapshot, momentum, bits, inner_v, res_a, res_b, mom_next, *scratch):
    n_z, n_y, chunks, share, wide = dims
    replicas, total = n_z * n_y, 2 * chunks
    frags = inner_v.shape[0]
    bbuf, snap, mom, acc_a, acc_b, wsem, bsem, ssem, msem = scratch[:9]
    refs_a, refs_b = (*scratch[9:14], res_a), (*scratch[14:19], res_b)
    sems_a, sems_b = scratch[19:31], scratch[31:43]
    me = lax.axis_index("replica")
    y, z = lax.rem(me, n_y), lax.div(me, n_y)
    groups = owners(n_z)
    strip = n_y * share

    def parts_at(r):
        line_y = Line(r % n_y, n_y, 1, r)
        line_z = Line(r // n_y, n_z, n_y, r)
        ctx = (snap, mom, mom_next)
        return (
            Part(refs_a, sems_a, line_y, line_z, (*ctx, acc_a, replicas, share, 0, wide), True),
            Part(refs_b, sems_b, line_y, line_z, (*ctx, acc_b, replicas, share, wide, share - wide), False),
        )

    def loads(rc, kind):
        i = 2 * rc + kind
        copies = []
        for slot, owner in enumerate(groups[kind]):
            cols = slice(owner * strip, (owner + 1) * strip)
            copies += [
                pltpu.make_async_copy(inner.at[0, :, rc, :, cols], inner_v.at[:, rc, :, cols], wsem.at[i, slot]),
                pltpu.make_async_copy(bits.at[rc, :, cols], bbuf.at[kind, slot], bsem.at[kind, slot]),
                pltpu.make_async_copy(snapshot.at[rc, :, cols], snap.at[rc, :, cols], ssem.at[i, slot]),
            ]
        return copies

    for copy in loads(0, 0):
        copy.start()
    mom_copy = pltpu.make_async_copy(momentum, mom, msem)

    barrier = pltpu.get_barrier_semaphore()
    count = 0
    for pos, n, step in ((y, n_y, 1), (z, n_z, n_y)):
        for delta, there in ((-step, pos > 0), (step, pos < n - 1)):
            @pl.when(there)
            def _():
                pl.semaphore_signal(barrier, inc=1, device_id={"replica": me + delta}, device_id_type=MESH)

            count = count + there.astype(jnp.int32)

    def round_chunk(rc, kind):
        @pl.when(rc + kind < chunks)
        def _():
            for copy in loads(rc + kind, 1 - kind):
                copy.start()

        for copy in loads(rc, kind):
            copy.wait()
        which = frag[0]
        i = 2 * rc + kind
        for slot, owner in enumerate(groups[kind]):
            for by in range(n_y):
                cols = slice(owner * strip + by * share, owner * strip + (by + 1) * share)
                chosen = inner_v[0, rc, :, cols]
                for f in range(1, frags):
                    chosen = jnp.where(which == f, inner_v[f, rc, :, cols], chosen)
                scaled = grid_scale * (snap[rc, :, cols].astype(jnp.float32) - chosen.astype(jnp.float32))
                lower = jnp.floor(scaled)
                drawn = bbuf[kind, slot, :, by * share : (by + 1) * share].astype(jnp.float32)
                raised = jnp.where(drawn < bit_levels * (scaled - lower), 1.0, 0.0)
                rounded = ((lower + raised) / grid_scale).astype(jnp.bfloat16)
                refs_a[0][i, by, slot] = rounded[:, :wide]
                refs_b[0][i, slot, by] = rounded[:, wide:]

    plan = order_of(n_y, n_z)
    split = [kind for kind, _, _, _ in plan].index(-1)
    last = max(lag for _, _, _, lag in plan)
    first = min(lag for kind, s, _, lag in plan if kind >= 0 and s == n_y - 1 + depth(n_z, groups[kind]))

    def at_my_place(todo):
        for r in range(replicas):
            pl.when(me == r)(functools.partial(todo, parts_at(r)))

    def entries_of(parity, entries):
        for kind, s, part, lag in entries:
            if (parity - lag - kind) % 2 == 0:
                yield (parity - lag - kind) // 2, kind, s, part

    def two_ticks(u, carry, parts):
        def run(entries):
            for ahead, some in itertools.groupby(entries, key=lambda e: e[0]):
                rc = u + ahead

                @pl.when(jnp.logical_and(rc >= 0, rc < chunks))
                def _():
                    for _, kind, s, part in some:
                        parts[part].stage(s, 2 * rc + kind, rc, kind)

        pl.when(u == first // 2)(mom_copy.wait)
        before, after = ([[*entries_of(parity, p)] for parity in (0, 1)] for p in (plan[:split], plan[split + 1 :]))
        run(before[0])
        pl.when(u < chunks)(functools.partial(round_chunk, u, 1))
        run(after[0] + before[1])
        pl.when(u + 1 < chunks)(functools.partial(round_chunk, u + 1, 0))
        run(after[1])
        return carry

    round_chunk(0, 0)
    mom_copy.start()
    pl.semaphore_wait(barrier, count)
    ticks = pl.cdiv(total + last, 2)

    def all_ticks(parts):
        lax.fori_loop(0, ticks, lambda u, carry: two_ticks(u, carry, parts), 0)

    at_my_place(all_ticks)

    def settle(parts):
        for part in parts:
            part.settle(chunks)

    at_my_place(settle)


def finish_kernel(frag, inner_v, res_a, res_b, mom_next, snap_out, mom_out, inner_out, snap_v, blend_v, mom_sem, pass_sem, snap_sem, blend_sem):
    frags, chunks = inner_v.shape[:2]
    n_y, n_z = res_a.shape[1], 2 * res_a.shape[2]
    wide = res_a.shape[4]
    share = wide + res_b.shape[4]
    which = frag[0]
    waits = [pltpu.make_async_copy(mom_next, mom_out, mom_sem)]
    for j in range(1, frags):
        other = lax.rem(which + j, frags)
        waits.append(pltpu.make_async_copy(inner_v.at[other], inner_out.at[0, other], pass_sem.at[j]))

    def puts(c):
        return (
            pltpu.make_async_copy(snap_v.at[c], snap_out.at[c], snap_sem.at[c]),
            pltpu.make_async_copy(blend_v.at[c], inner_out.at[0, which, c], blend_sem.at[c]),
        )

    for copy in waits:
        copy.start()

    def blend(c, carry):
        for kind, group in enumerate(owners(n_z)):
            i = 2 * c + kind
            for slot, by in ((slot, by) for slot in range(len(group)) for by in range(n_y)):
                first = (group[slot] * n_y + by) * share
                for col, part in ((first, res_a[i, by, slot]), (first + wide, res_b[i, slot, by])):
                    cols = slice(col, col + part.shape[1])
                    snap_v[c, :, cols] = part
                    blend_v[c, :, cols] = (
                        blend_keep * inner_v[which, c, :, cols].astype(jnp.float32)
                        + (1.0 - blend_keep) * part.astype(jnp.float32)
                    ).astype(jnp.bfloat16)
        for copy in puts(c):
            copy.start()
        return carry

    lax.fori_loop(0, chunks, blend, 0)
    for copy in waits:
        copy.wait()

    def settle(c, carry):
        for copy in puts(c):
            copy.wait()
        return carry

    lax.fori_loop(0, chunks, settle, 0)


def body(inner_weights, snapshot, momentum, rand_bits, fragment):
    n = lax.axis_size("replica")
    outer, inner_n = grid_of(n)
    frags, rows, width = inner_weights.shape[1:]
    share = momentum.shape[1]
    wide = max(1, min(share // 128 - 1, round(0.6 * share / 128))) * 128
    narrow = share - wide
    chunks = rows // CHUNK_ROWS
    bf, f32 = jnp.bfloat16, jnp.float32
    dma = pltpu.SemaphoreType.DMA

    half, total = outer // 2, 2 * chunks

    def bufs(w, y_first):
        block = (CHUNK_ROWS, w)
        own = (total, inner_n, half, *block) if y_first else (total, half, inner_n, *block)
        line_y = own if y_first else (total, inner_n, *block)
        line_z = (total, half, *block) if y_first else own
        return [pltpu.VMEM(s, bf) for s in (own, line_y, line_y, line_z, line_z)]

    def sems():
        on_y, on_z = (total, inner_n), (total, half)
        one, two = (1,), (2,)
        return [dma(s) for s in (one, on_y, on_y, two, on_z, on_z, on_y, one, one, on_z, two, two)]

    scratch = [
        pltpu.VMEM((2, half, CHUNK_ROWS, inner_n * share), jnp.int32),
        pltpu.VMEM((chunks, CHUNK_ROWS, width), bf),
        pltpu.VMEM((chunks, CHUNK_ROWS, share), f32),
        pltpu.VMEM((CHUNK_ROWS, wide), f32),
        pltpu.VMEM((CHUNK_ROWS, narrow), f32),
        dma((total, half)), dma((2, half)), dma((total, half)), dma,
        *bufs(wide, True), *bufs(narrow, False),
        *sems(), *sems(),
    ]
    anywhere = pl.BlockSpec(memory_space=pl.ANY)
    in_vmem = pl.BlockSpec(memory_space=pltpu.VMEM)
    in_smem = pl.BlockSpec(memory_space=pltpu.SMEM)
    held = pl.pallas_call(
        functools.partial(exchange_kernel, (outer, inner_n, chunks, share, wide)),
        out_shape=(
            pltpu.VMEM((frags, chunks, CHUNK_ROWS, width), bf),
            pltpu.VMEM((total, inner_n, half, CHUNK_ROWS, wide), bf),
            pltpu.VMEM((total, half, inner_n, CHUNK_ROWS, narrow), bf),
            pltpu.VMEM((chunks, CHUNK_ROWS, share), f32),
        ),
        in_specs=[in_smem] + [pl.BlockSpec(memory_space=pltpu.HBM)] * 4,
        out_specs=(in_vmem,) * 4,
        scratch_shapes=scratch,
        compiler_params=pltpu.CompilerParams(
            collective_id=0, has_side_effects=True, vmem_limit_bytes=EXCHANGE_VMEM
        ),
        name="exchange",
    )(
        fragment,
        inner_weights.reshape(1, frags, chunks, CHUNK_ROWS, width),
        snapshot.reshape(chunks, CHUNK_ROWS, width),
        momentum.reshape(chunks, CHUNK_ROWS, share),
        rand_bits.reshape(chunks, CHUNK_ROWS, width),
    )

    new_snapshot, new_momentum, new_inner = pl.pallas_call(
        finish_kernel,
        in_specs=[in_smem] + [in_vmem] * 4,
        out_specs=(anywhere,) * 3,
        out_shape=(
            jax.ShapeDtypeStruct((chunks, CHUNK_ROWS, width), bf),
            jax.ShapeDtypeStruct((chunks, CHUNK_ROWS, share), f32),
            jax.ShapeDtypeStruct((1, frags, chunks, CHUNK_ROWS, width), bf),
        ),
        scratch_shapes=[
            pltpu.VMEM((chunks, CHUNK_ROWS, width), bf),
            pltpu.VMEM((chunks, CHUNK_ROWS, width), bf),
            dma, dma((frags,)), dma((chunks,)), dma((chunks,)),
        ],
        compiler_params=pltpu.CompilerParams(vmem_limit_bytes=FINISH_VMEM),
        name="finish",
    )(fragment, *held)
    return new_snapshot.reshape(rows, width), new_momentum.reshape(rows, share), new_inner.reshape(inner_weights.shape)


def solution(mesh):
    placed = (
        P("replica", None, "fsdp", None),
        P("fsdp", None),
        P("fsdp", "replica"),
        P("replica", "fsdp", None),
        P(),
    )
    return jax.shard_map(
        body,
        mesh=mesh,
        in_specs=placed,
        out_specs=(P("fsdp", None), P("fsdp", "replica"), P("replica", None, "fsdp", None)),
        check_vma=False,
    )
```
